256 devices in a mesh: grp: 2 (over x_hi), row: 16 (over z, core), col: 8 (over y, x_lo).
Axes of the slice: x: 4 (x_hi: 2, x_lo: 2; x = x_hi * 2 + x_lo), y: 4, z: 8, core: 2. Of those that a mesh axis runs over, the one named last changes fastest.
Arguments:
- vectors: float32 [64, 256, 2048], P('grp', 'row', 'col'), may hold values from -6 to 6
- disorder: float32 [256, 2048], P('row', 'col'), may hold values from -1.5 to 1.5
Outputs:
- cheb_prev: float32 [64, 256, 2048], P('grp', 'row', 'col')
- cheb_last: float32 [64, 256, 2048], P('grp', 'row', 'col')
- moments: float32 [17], replicated
The draws below stay inside these ranges and needn't reach their ends.
All inputs are finite; a program needn't handle non-finite values.
Results may differ from the reference program's by a relative error of at most 0.0001.
Values sent between devices are 32-bit elements; how exact they have to be, the bound alone decides.
A program may use at most 64 MiB of HBM per device.

```python
import jax
import jax.numpy as jnp
from jax import lax

STEPS = 8
V_ALL = 64
NR = 256
NC = 2048


def shard_levels(key, extent, cuts, least, high):
    level, own = 1.0, jax.random.fold_in(key, 6)
    for dim, blocks in cuts:
        steps = jnp.exp(jax.random.uniform(jax.random.fold_in(own, dim), (blocks,), jnp.float32, least / len(cuts), high / len(cuts)))
        level = level * jnp.repeat(steps, extent[dim] // blocks).reshape([-1 if axis == dim else 1 for axis in range(len(extent))])
    return level


def centred(own_key, dims, width, reach, split=(), held_as=jnp.bfloat16):
    result = jax.random.normal(own_key, dims, jnp.float32) * width
    if len(split) > 0:
        result = shard_levels(own_key, dims, split, -0.22, 0.18) * result
    return jnp.clip(result, min=-reach, max=reach).astype(held_as)


def setup_inputs(seed: int = 0) -> dict:
    seeds = jax.random.split(jax.random.key(seed), 3)
    vectors = centred(seeds[0], (V_ALL, NR, NC), 1.0, 6.0, ((0, 2), (1, 16), (2, 8)), jnp.float32)
    disorder = jnp.clip(jax.random.uniform(seeds[1], (NR, NC), jnp.float32, -1.5, 1.5) * shard_levels(seeds[1], (NR, NC), ((0, 16), (1, 8)), -0.4, 0.0), -1.5, 1.5)
    return {"vectors": vectors, "disorder": disorder}


SCALE = 4.6


def hop(field, disorder, even):
    below = jnp.roll(field, -1, 0)
    above = jnp.roll(field, 1, 0)
    left = jnp.roll(field, 1, 1)
    right = jnp.roll(field, -1, 1)
    vertical = jnp.where(even, below, above)
    return (disorder * field - (left + right + vertical)) / SCALE


def reference(vectors, disorder):
    rows = lax.broadcasted_iota(jnp.int32, (NR, NC), 0)
    cols = lax.broadcasted_iota(jnp.int32, (NR, NC), 1)
    even = (rows + cols) % 2 == 0

    def single(vector):
        older = vector
        newer = hop(vector, disorder, even)
        squares = [jnp.sum(older * older), jnp.sum(newer * newer)]
        crosses = [jnp.sum(newer * older)]
        for step in range(1, STEPS):
            latest = 2.0 * hop(newer, disorder, even) - older
            squares.append(jnp.sum(latest * latest))
            crosses.append(jnp.sum(latest * newer))
            older, newer = newer, latest
        return older, newer, jnp.stack(squares), jnp.stack(crosses)

    older, newer, squares, crosses = lax.map(single, vectors)
    count = float(V_ALL * NR * NC)
    squares = jnp.sum(squares, axis=0) / count
    crosses = jnp.sum(crosses, axis=0) / count
    first = squares[0]
    second = crosses[0]
    values = [first, second]
    for index in range(1, STEPS + 1):
        values.append(2.0 * squares[index] - first)
        if index < STEPS:
            values.append(2.0 * crosses[index] - second)
    return older, newer, jnp.stack(values).astype(jnp.float32)
```

```python
import functools

import jax
import jax.numpy as jnp
from jax import lax
from jax.experimental import pallas as pl
from jax.experimental.pallas import tpu as pltpu
from jax.sharding import PartitionSpec as P

STEPS = 8
SCALE = 4.6
COUPLING = 2.0 / SCALE
MESH = pl.DeviceIdType.MESH
NQ = 2 * STEPS + 1
NV, RH, CH = 32, 16, 256
PAD = (STEPS + 1) // 2
ROWS = RH + 2 * PAD
SLOTS = NV // 8
SW = 128 // SLOTS
WIDE = STEPS


def roll(x, shift):
    return pltpu.roll(x, shift % 128, axis=x.ndim - 1)


def lanes(shape):
    return lax.broadcasted_iota(jnp.int32, shape, len(shape) - 1)


def kernel(
    sizes, vec_hbm, dis_hbm, prev_out, last_out, mom_out,
    V, F, S, DE, DB, PK, RC, ACC, R1, R2,
    load_sem, out_sem, send_sem, recv_sem, s1_send, s1_recv, s2_send, s2_recv,
):
    GR, ROW, COL = sizes
    COUNT = float(GR * NV * ROW * RH * COL * CH)
    g = lax.axis_index("grp")
    r = lax.axis_index("row")
    c = lax.axis_index("col")
    up, down = lax.rem(r + ROW - 1, ROW), lax.rem(r + 1, ROW)
    left, right = lax.rem(c + COL - 1, COL), lax.rem(c + 1, COL)

    sites = pl.ds(0, NV * RH)
    loads = [
        pltpu.make_async_copy(
            vec_hbm.at[:, pl.ds(128 * h, 128)], V.at[h, sites], load_sem.at[h]
        )
        for h in range(2)
    ]
    loads.append(
        pltpu.make_async_copy(
            dis_hbm, DE.at[pl.ds(8, RH), pl.ds(128, CH)], load_sem.at[2]
        )
    )
    for copy in loads:
        copy.start()

    row_peers = [(g, lax.rem(r + d, ROW), c) for d in range(1, ROW)]
    col_peers = []
    for dg in range(GR):
        for dc in range(COL):
            if dg or dc:
                col_peers.append((lax.rem(g + dg, GR), r, lax.rem(c + dc, COL)))
    corners = [(g, a, b) for a in (up, down) for b in (left, right)]
    barrier = pltpu.get_barrier_semaphore()
    for peer in row_peers + col_peers + corners:
        pl.semaphore_signal(barrier, inc=1, device_id=peer, device_id_type=MESH)

    for copy in loads:
        copy.wait()

    lane8 = lanes((8, 128))
    slot8 = lane8 // SW
    in8 = lane8 % SW

    def own_strips(row):
        m0 = F[0, row, :, 0:128]
        m1 = F[0, row, :, 128:256]
        xl = jnp.zeros((8, 128), jnp.float32)
        xr = jnp.zeros((8, 128), jnp.float32)
        for t in range(SLOTS):
            ml = (slot8 == t) & (in8 >= WIDE) & (in8 < 3 * WIDE)
            mr = (slot8 == t) & (in8 < 2 * WIDE)
            xl = jnp.where(ml, roll(m0[8 * t : 8 * t + 8], SW * t + WIDE), xl)
            xr = jnp.where(mr, roll(m1[8 * t : 8 * t + 8], SW * t + 2 * WIDE), xr)
        return xl, xr

    def strided(i, t):
        return pl.ds(t * 8 * RH + i, 8, stride=RH)

    for i in range(RH):
        for t in range(SLOTS):
            for h in range(2):
                F[0, PAD + i, 8 * t : 8 * t + 8, 128 * h : 128 * h + 128] = V.at[h][
                    strided(i, t), :
                ]

    def pack(a, _):
        pleft = jnp.zeros((8, 128), jnp.float32)
        pright = jnp.zeros((8, 128), jnp.float32)
        for b in range(4):
            row = PAD + 4 * a + b
            xl, xr = own_strips(row)
            S[0, row, :, 0:128] = xl
            S[0, row, :, 128:256] = xr
            m = (in8 // WIDE) == b
            pleft = jnp.where(m, roll(xl, WIDE * b - WIDE), pleft)
            pright = jnp.where(m, roll(xr, WIDE * b - WIDE), pright)
        PK[0, a] = pleft
        PK[1, a] = pright
        return 0

    lax.fori_loop(0, RH // 4, pack, 0)

    pl.semaphore_wait(barrier, len(row_peers) + len(col_peers) + len(corners))

    mid = pl.ds(128, CH)
    plan = [
        (F.at[0, pl.ds(PAD + RH - PAD, PAD)], F.at[0, pl.ds(0, PAD)], (g, down, c)),
        (F.at[0, pl.ds(PAD, PAD)], F.at[0, pl.ds(PAD + RH, PAD)], (g, up, c)),
        (PK.at[1], RC.at[0, pl.ds(1, 4)], (g, r, right)),
        (PK.at[0], RC.at[1, pl.ds(1, 4)], (g, r, left)),
        (PK.at[1, 3], RC.at[0, 0], (g, down, right)),
        (PK.at[1, 0], RC.at[0, 5], (g, up, right)),
        (PK.at[0, 3], RC.at[1, 0], (g, down, left)),
        (PK.at[0, 0], RC.at[1, 5], (g, up, left)),
        (DE.at[pl.ds(16, 8), mid], DE.at[pl.ds(0, 8), mid], (g, down, c)),
        (DE.at[pl.ds(8, 8), mid], DE.at[pl.ds(24, 8), mid], (g, up, c)),
        (DE.at[pl.ds(8, 16), pl.ds(256, 128)], DE.at[pl.ds(8, 16), pl.ds(0, 128)], (g, r, right)),
        (DE.at[pl.ds(8, 16), pl.ds(128, 128)], DE.at[pl.ds(8, 16), pl.ds(384, 128)], (g, r, left)),
        (DE.at[pl.ds(16, 8), pl.ds(256, 128)], DE.at[pl.ds(0, 8), pl.ds(0, 128)], (g, down, right)),
        (DE.at[pl.ds(8, 8), pl.ds(256, 128)], DE.at[pl.ds(24, 8), pl.ds(0, 128)], (g, up, right)),
        (DE.at[pl.ds(16, 8), pl.ds(128, 128)], DE.at[pl.ds(0, 8), pl.ds(384, 128)], (g, down, left)),
        (DE.at[pl.ds(8, 8), pl.ds(128, 128)], DE.at[pl.ds(24, 8), pl.ds(384, 128)], (g, up, left)),
    ]
    halo = [
        pltpu.make_async_remote_copy(
            src_ref=source, dst_ref=target, send_sem=send_sem.at[k], recv_sem=recv_sem.at[k],
            device_id=device, device_id_type=MESH,
        )
        for k, (source, target, device) in enumerate(plan)
    ]
    order = [2, 3, 4, 5, 6, 7, 0, 1] + list(range(8, 16))
    for k in order:
        halo[k].start()

    first_lane = lane8 == 0
    last_lane = lane8 == 127
    even_lane = lane8 % 2 == 0

    def spread_loop(lo, hi):
        for q in range(4):
            rows = [i for i in range(8) if lo <= 8 * q + i - (8 - PAD) < hi]
            if rows:
                x = DE[8 * q : 8 * q + 8, 128:384] * COUPLING
            for i in rows:
                DB[8 * q + i - (8 - PAD), :, 0:256] = jnp.broadcast_to(x[i : i + 1], (8, 256))

    spread_loop(PAD, PAD + RH)

    def update(level, c, vert, old, d, wide):
        if wide:
            c0, c1 = c
            l0 = roll(c0, 1)
            r1 = roll(c1, -1)
            l1 = jnp.where(first_lane, l0, roll(c1, 1))
            r0 = jnp.where(last_lane, r1, roll(c0, -1))
            sides = (l0 + r0, l1 + r1)
        else:
            sides = tuple(roll(x, 1) + roll(x, -1) for x in c)
        out = []
        for k in range(2):
            new = d[k] * c[k] - COUPLING * (sides[k] + vert[k])
            new = 0.5 * new if level == 1 else new - old[k]
            out.append(new)
        return out

    def halves(ref, level, row, t=None):
        if t is None:
            return ref[level, row, :, 0:128], ref[level, row, :, 128:256]
        return ref[level, row, 8 * t : 8 * t + 8, 0:128], ref[level, row, 8 * t : 8 * t + 8, 128:256]

    def one_row(level, row, mask, main, strip, acc):
        if acc is not None:
            acc = list(acc)

        def vertical(ref, t):
            if mask is True:
                return halves(ref, level - 1, row + 1, t)
            if mask is False:
                return halves(ref, level - 1, row - 1, t)
            below = halves(ref, level - 1, row + 1, t)
            above = halves(ref, level - 1, row - 1, t)
            return [jnp.where(mask, below[k], above[k]) for k in range(2)]

        if main:
            d = DB[row, :, 0:128], DB[row, :, 128:256]
            for t in range(SLOTS):
                c = halves(F, level - 1, row, t)
                old = halves(F, level - 2, row, t) if level > 1 else None
                new = update(level, c, vertical(F, t), old, d, True)
                for k in range(2):
                    F[level, row, 8 * t : 8 * t + 8, 128 * k : 128 * k + 128] = new[k]
                    if acc is not None:
                        acc[k] = acc[k] + new[k] * new[k]
                        acc[2 + k] = acc[2 + k] + new[k] * c[k]
        if strip:
            d = DB[row, :, 256:384], DB[row, :, 384:512]
            c = halves(S, level - 1, row)
            old = halves(S, level - 2, row) if level > 1 else None
            new = update(level, c, vertical(S, None), old, d, False)
            for k in range(2):
                S[level, row, :, 128 * k : 128 * k + 128] = new[k]
                if acc is not None:
                    acc[4 + k] = acc[4 + k] + new[k] * new[k]
                    acc[6 + k] = acc[6 + k] + new[k] * c[k]
        return acc

    def parity(row):
        return (lane8 + row) % 2 == 0

    zero = jnp.zeros((8, 128), jnp.float32)
    accs = [[zero] * 8 for _ in range(STEPS + 1)]

    def square0(i, acc):
        acc = list(acc)
        for t in range(SLOTS):
            x = halves(F, 0, i, t)
            for k in range(2):
                acc[k] = acc[k] + x[k] * x[k]
        return tuple(acc)

    a0 = lax.fori_loop(PAD, PAD + RH, square0, (zero, zero), unroll=2)
    accs[0][0:2] = a0

    for n in range(1, STEPS + 1):
        edge = (n + 1) // 2
        lo = PAD + edge
        if n % 2:
            one_row(n, lo - 1, True, True, False, None)
            one_row(n, PAD + RH - edge, False, True, False, None)

        def pair(j, acc, n=n, lo=lo):
            for u in range(2):
                row = lo + 2 * j + u
                mask = even_lane if (lo + u) % 2 == 0 else jnp.logical_not(even_lane)
                acc = one_row(n, row, mask, True, False, tuple(acc) + (zero,) * 4)[:4]
            return tuple(acc)

        a = lax.fori_loop(0, (RH - 2 * edge) // 2, pair, (zero,) * 4)
        accs[n][0:4] = a

    for k in range(16):
        halo[k].wait_recv()

    spread_loop(0, PAD)
    spread_loop(PAD + RH, ROWS)

    for q in range(4):
        for side in range(2):
            rows = pl.ds(8 * q, 8)
            if side == 0:
                a, b = DE[rows, 0:128], DE[rows, 128:256]
                x = jnp.where(lane8 < WIDE, roll(a, WIDE), roll(b, WIDE))
            else:
                a, b = DE[rows, 256:384], DE[rows, 384:512]
                x = jnp.where(lane8 < 2 * WIDE, roll(a, 2 * WIDE), roll(b, 2 * WIDE))
            x = jnp.where(lane8 < 3 * WIDE, x * COUPLING, 0.0)
            x = x + roll(x, SW)
            x = x + roll(x, 2 * SW)
            for i in range(8):
                row = 8 * q + i - (8 - PAD)
                if 0 <= row < ROWS:
                    DB[row, :, 256 + 128 * side : 384 + 128 * side] = jnp.broadcast_to(
                        x[i : i + 1], (8, 128)
                    )

    def strips(a, own):
        gl, gr = RC[0, a], RC[1, a]
        for b in range(4):
            row = 4 * a + b
            if own:
                xl, xr = own_strips(row)
            else:
                xl, xr = halves(S, 0, row)
            xl = jnp.where(in8 < WIDE, roll(gl, -WIDE * b), xl)
            xr = jnp.where(
                (in8 >= 2 * WIDE) & (in8 < 3 * WIDE), roll(gr, 2 * WIDE - WIDE * b), xr
            )
            S[0, row, :, 0:128] = xl
            S[0, row, :, 128:256] = xr

    strips(0, True)
    strips(5, True)

    def strips_mid(a, _):
        strips(a, False)
        return 0

    lax.fori_loop(1, 5, strips_mid, 0)

    for n in range(1, STEPS + 1):
        edge = (n + 1) // 2
        reach = (STEPS + 1 - n) // 2
        top, bottom = PAD - reach, PAD + RH - 1 + reach
        if n % 2:
            one_row(n, top, True, True, True, None)
            one_row(n, bottom, False, True, True, None)
            top += 1

        def outside(i, _, n=n):
            one_row(n, i, parity(i), True, True, None)
            j = ROWS - 1 - i
            one_row(n, j, parity(j), True, True, None)
            return 0

        if top < PAD:
            lax.fori_loop(top, PAD, outside, 0)

        def inside(i, acc, n=n):
            acc = one_row(n, i, parity(i), True, True, acc)
            j = ROWS - 1 - i
            return tuple(one_row(n, j, parity(j), True, True, acc))

        acc = tuple(accs[n])
        acc = lax.fori_loop(PAD, PAD + edge, inside, acc)

        def middle(i, acc, n=n, lo=PAD + edge):
            acc = tuple(acc)
            for u in range(2):
                row = lo + 2 * i + u
                mask = even_lane if (lo + u) % 2 == 0 else jnp.logical_not(even_lane)
                acc = one_row(n, row, mask, False, True, (zero,) * 4 + tuple(acc))[4:]
            return tuple(acc)

        rest = lax.fori_loop(0, (RH - 2 * edge) // 2, middle, acc[4:])
        accs[n] = list(acc[:4]) + list(rest)

    base = []
    for n in range(STEPS + 1):
        own = [
            lane8 >= n,
            lane8 < 128 - n,
            (in8 >= WIDE) & (in8 < WIDE + n),
            (in8 >= 2 * WIDE - n) & (in8 < 2 * WIDE),
        ]
        for kind in range(2):
            if n == 0 and kind == 1:
                continue
            total = zero
            picks = (0, 1, 4, 5) if kind == 0 else (2, 3, 6, 7)
            for m, k in zip(own, picks):
                if n == 0:
                    total = total + accs[n][k]
                else:
                    total = total + jnp.where(m, accs[n][k], 0.0)
            q = 2 * n if kind == 0 else 2 * n - 1
            if q < 2:
                base.append(total)
            else:
                total = 2.0 * total - base[q % 2]
            ACC[q] = total
    for q in range(NQ, 24):
        ACC[q] = zero
    sums = jnp.sum(ACC[...], axis=1)
    totals = jnp.broadcast_to(jnp.sum(sums, axis=1, keepdims=True), (24, 128))
    at = lax.broadcasted_iota(jnp.int32, (24, 128), 0) == lanes((24, 128))
    R1[r] = jnp.sum(jnp.where(at, totals, 0.0), axis=0, keepdims=True)

    def exchange(buf, mine, peers, send, recv):
        return [
            pltpu.make_async_remote_copy(
                src_ref=buf.at[mine], dst_ref=buf.at[mine],
                send_sem=send.at[k], recv_sem=recv.at[k],
                device_id=peer, device_id_type=MESH,
            )
            for k, peer in enumerate(peers)
        ]

    first = exchange(R1, r, row_peers, s1_send, s1_recv)
    for copy in first:
        copy.start()

    for k, level in enumerate((STEPS - 1, STEPS)):
        for i in range(RH):
            xl, xr = halves(S, level, PAD + i)
            for t in range(SLOTS):
                m0, m1 = halves(F, level, PAD + i, t)
                V.at[2 * k][strided(i, t), :] = jnp.where(
                    lane8 < WIDE, roll(xl, -(SW * t + WIDE)), m0
                )
                V.at[2 * k + 1][strided(i, t), :] = jnp.where(
                    lane8 >= 128 - WIDE, roll(xr, 128 - 2 * WIDE - SW * t), m1
                )
    outs = [
        pltpu.make_async_copy(
            V.at[2 * k + h, sites], ref.at[:, pl.ds(128 * h, 128)], out_sem.at[k, h]
        )
        for k, ref in enumerate((prev_out, last_out))
        for h in range(2)
    ]
    for copy in outs:
        copy.start()

    for copy in first:
        copy.wait_recv()
    mine = g * COL + c
    R2[mine] = jnp.sum(R1[...], axis=0)
    second = exchange(R2, mine, col_peers, s2_send, s2_recv)
    for copy in second:
        copy.start()
    for copy in second:
        copy.wait_recv()
    mom_out[...] = jnp.sum(R2[...], axis=0) * (1.0 / COUNT)

    for copy in halo + first + second:
        copy.wait_send()
    for copy in outs:
        copy.wait()


def body(sizes, vectors, disorder):
    GR, ROW, COL = sizes
    f32 = jnp.float32
    dma = pltpu.SemaphoreType.DMA
    hbm = pl.BlockSpec(memory_space=pltpu.HBM)
    prev, last, moments = pl.pallas_call(
        functools.partial(kernel, sizes),
        out_shape=(
            jax.ShapeDtypeStruct((NV * RH, CH), f32),
            jax.ShapeDtypeStruct((NV * RH, CH), f32),
            jax.ShapeDtypeStruct((1, 128), f32),
        ),
        in_specs=[hbm, hbm],
        out_specs=(hbm, hbm, pl.BlockSpec(memory_space=pltpu.VMEM)),
        scratch_shapes=[
            pltpu.VMEM((4, (NV + 1) * RH, 128), f32),
            pltpu.VMEM((STEPS + 1, ROWS, NV, CH), f32),
            pltpu.VMEM((STEPS + 1, ROWS, 8, 256), f32),
            pltpu.VMEM((32, 512), f32),
            pltpu.VMEM((ROWS, 8, 512), f32),
            pltpu.VMEM((2, 4, 8, 128), f32),
            pltpu.VMEM((2, 6, 8, 128), f32),
            pltpu.VMEM((24, 8, 128), f32),
            pltpu.VMEM((ROW, 1, 128), f32),
            pltpu.VMEM((GR * COL, 1, 128), f32),
            dma((3,)),
            dma((2, 2)),
            dma((16,)),
            dma((16,)),
            dma((ROW - 1,)),
            dma((ROW - 1,)),
            dma((GR * COL - 1,)),
            dma((GR * COL - 1,)),
        ],
        compiler_params=pltpu.CompilerParams(
            collective_id=0, has_side_effects=True, vmem_limit_bytes=32 << 20
        ),
    )(vectors.reshape(NV * RH, CH), disorder)
    return prev.reshape(vectors.shape), last.reshape(vectors.shape), moments[0, :NQ]


def solution(mesh):
    sizes = mesh.shape["grp"], mesh.shape["row"], mesh.shape["col"]
    return jax.shard_map(
        functools.partial(body, sizes),
        mesh=mesh,
        in_specs=(P("grp", "row", "col"), P("row", "col")),
        out_specs=(P("grp", "row", "col"), P("grp", "row", "col"), P()),
        check_vma=False,
    )
```

```python
import functools

import jax
import jax.numpy as jnp
from jax import lax
from jax.experimental import pallas as pl
from jax.experimental.pallas import tpu as pltpu
from jax.sharding import PartitionSpec as P

STEPS = 8
SCALE = 4.6
COUPLING = 2.0 / SCALE
MESH = pl.DeviceIdType.MESH
NQ = 2 * STEPS + 1
NV, RH, CH = 32, 16, 256
PAD = (STEPS + 1) // 2
ROWS = RH + 2 * PAD
SLOTS = NV // 8


def roll(x, shift):
    return pltpu.roll(x, shift % 128, axis=1)


def gather(x, index):
    return jnp.take_along_axis(x, index, axis=1, mode="promise_in_bounds")


def half_of(i, kind):
    return (i + kind) % 2


def alone(i, kind, n):
    j = RH - 1 - i
    return n <= (min(2 * i + 1, 2 * j) if kind == 0 else min(2 * i, 2 * j + 1))


def wanted(i, kind, n):
    if i < 0:
        return n <= STEPS + 1 + 2 * i - kind
    if i >= RH:
        return n <= STEPS + 1 - 2 * (i - RH + 1) - (1 - kind)
    return True


def kernel(
    sizes, vec_hbm, dis_hbm, prev_out, last_out, mom_out,
    V, F, S, DE, DB, PK, RC, ACC, SUM, R1, R2,
    load_sem, out_sem, send_sem, recv_sem, s1_send, s1_recv, s2_send, s2_recv,
):
    GR, ROW, COL = sizes
    COUNT = float(GR * NV * ROW * RH * COL * CH)
    g = lax.axis_index("grp")
    r = lax.axis_index("row")
    c = lax.axis_index("col")
    up, down = lax.rem(r + ROW - 1, ROW), lax.rem(r + 1, ROW)
    left, right = lax.rem(c + COL - 1, COL), lax.rem(c + 1, COL)

    sites = pl.ds(0, NV * RH)
    loads = [
        pltpu.make_async_copy(
            vec_hbm.at[:, pl.ds(128 * h, 128)], V.at[h, sites], load_sem.at[h]
        )
        for h in range(2)
    ]
    loads.append(
        pltpu.make_async_copy(
            dis_hbm, DE.at[pl.ds(8, RH), pl.ds(128, CH)], load_sem.at[2]
        )
    )
    for copy in loads:
        copy.start()

    row_peers = [(g, lax.rem(r + d, ROW), c) for d in range(1, ROW)]
    col_peers = []
    for dg in range(GR):
        for dc in range(COL):
            if dg or dc:
                col_peers.append((lax.rem(g + dg, GR), r, lax.rem(c + dc, COL)))
    corners = [(g, a, b) for a in (up, down) for b in (left, right)]
    barrier = pltpu.get_barrier_semaphore()
    for peer in row_peers + col_peers + corners:
        pl.semaphore_signal(barrier, inc=1, device_id=peer, device_id_type=MESH)

    lane = lax.broadcasted_iota(jnp.int32, (8, 128), 1)
    zero = jnp.zeros((8, 128), jnp.float32)
    in16 = lane % 16
    in32 = lane % 32
    is_left = in32 < 16
    low = lane < 64
    pick = ((2 * lane) % 128, (2 * lane + 1) % 128)

    for copy in loads:
        copy.wait()

    def strided(i, t):
        return pl.ds(t * 8 * RH + i, 8, stride=RH)

    def split(m0, m1):
        return [jnp.where(low, gather(m0, p), gather(m1, p)) for p in pick]

    def get(ref, n, row, t, h):
        return ref[n, row, t, :, 128 * h : 128 * h + 128]

    def put(ref, n, row, t, h, x):
        ref[n, row, t, :, 128 * h : 128 * h + 128] = x

    strip_index = jnp.where(
        is_left, jnp.clip(in16 - 4, 0, 127), jnp.clip(120 + in16, 0, 127)
    )
    strip_own = (is_left & (in16 >= 4) & (in16 < 12)) | (~is_left & (in16 < 8))

    def own_strip(parts):
        x = gather(parts[0], strip_index)
        for t in range(1, SLOTS):
            x = jnp.where(lane >= 32 * t, gather(parts[t], strip_index), x)
        return jnp.where(strip_own, x, 0.0)

    order = [0, 1, 2, 3, 12, 13, 14, 15] + list(range(4, 12))
    packed = {}
    for i in order:
        parts = ([], [])
        for t in range(SLOTS):
            halves = split(V.at[0][strided(i, t), :], V.at[1][strided(i, t), :])
            for h in range(2):
                put(F, 0, PAD + i, t, h, halves[h])
                parts[h].append(halves[h])
        for h in range(2):
            x = own_strip(parts[h])
            put(S, 0, PAD + i, 0, h, x)
            a, spot = i // 4, 4 * (2 * (i % 4) + h)
            m = (in32 >= spot) & (in32 < spot + 4)
            for side, edge in ((0, 4), (1, 20)):
                packed[side, a] = jnp.where(m, roll(x, spot - edge), packed.get((side, a), zero))
                if i % 4 == 3 and h == 1:
                    PK[side, a] = packed[side, a]

    pl.semaphore_wait(barrier, len(row_peers) + len(col_peers) + len(corners))

    mid = pl.ds(128, CH)
    plan = [
        (F.at[0, pl.ds(PAD + RH - PAD, PAD)], F.at[0, pl.ds(0, PAD)], (g, down, c)),
        (F.at[0, pl.ds(PAD, PAD)], F.at[0, pl.ds(PAD + RH, PAD)], (g, up, c)),
        (PK.at[1], RC.at[0, pl.ds(1, 4)], (g, r, right)),
        (PK.at[0], RC.at[1, pl.ds(1, 4)], (g, r, left)),
        (PK.at[1, 3], RC.at[0, 0], (g, down, right)),
        (PK.at[1, 0], RC.at[0, 5], (g, up, right)),
        (PK.at[0, 3], RC.at[1, 0], (g, down, left)),
        (PK.at[0, 0], RC.at[1, 5], (g, up, left)),
        (DE.at[pl.ds(16, 8), mid], DE.at[pl.ds(0, 8), mid], (g, down, c)),
        (DE.at[pl.ds(8, 8), mid], DE.at[pl.ds(24, 8), mid], (g, up, c)),
        (DE.at[pl.ds(8, 16), pl.ds(256, 128)], DE.at[pl.ds(8, 16), pl.ds(0, 128)], (g, r, right)),
        (DE.at[pl.ds(8, 16), pl.ds(128, 128)], DE.at[pl.ds(8, 16), pl.ds(384, 128)], (g, r, left)),
        (DE.at[pl.ds(16, 8), pl.ds(256, 128)], DE.at[pl.ds(0, 8), pl.ds(0, 128)], (g, down, right)),
        (DE.at[pl.ds(8, 8), pl.ds(256, 128)], DE.at[pl.ds(24, 8), pl.ds(0, 128)], (g, up, right)),
        (DE.at[pl.ds(16, 8), pl.ds(128, 128)], DE.at[pl.ds(0, 8), pl.ds(384, 128)], (g, down, left)),
        (DE.at[pl.ds(8, 8), pl.ds(128, 128)], DE.at[pl.ds(24, 8), pl.ds(384, 128)], (g, up, left)),
    ]
    halo = [
        pltpu.make_async_remote_copy(
            src_ref=source, dst_ref=target, send_sem=send_sem.at[k], recv_sem=recv_sem.at[k],
            device_id=device, device_id_type=MESH,
        )
        for k, (source, target, device) in enumerate(plan)
    ]
    for k in [0, 1, 4, 5, 6, 7, 2, 3] + list(range(8, 16)):
        halo[k].start()

    def spread_main(lo, hi):
        for q in range(4):
            rows = [i for i in range(8) if lo <= 8 * q + i - 8 < hi]
            if rows:
                x = split(DE[8 * q : 8 * q + 8, 128:256], DE[8 * q : 8 * q + 8, 256:384])
                for h in range(2):
                    y = x[h] * COUPLING
                    for i in rows:
                        DB[8 * q + i - 8 + PAD, :, 128 * h : 128 * h + 128] = jnp.broadcast_to(
                            y[i : i + 1], (8, 128)
                        )

    spread_main(0, RH)

    def advance(ref, n, row, t, kind, d, acc):
        h = half_of(row, kind)
        centre = get(ref, n - 1, row, t, h)
        other = get(ref, n - 1, row, t, 1 - h)
        bond = get(ref, n - 1, row + 1 - 2 * kind, t, h)
        around = other + roll(other, 1 if h == 0 else -1) + bond
        new = d(h) * centre - COUPLING * around
        new = 0.5 * new if n == 1 else new - get(ref, n - 2, row, t, h)
        put(ref, n, row, t, h, new)
        if acc is not None:
            acc[h] = acc[h] + new * new
            acc[2 + h] = acc[2 + h] + new * centre

    def main_d(row):
        return lambda h: DB[row, :, 128 * h : 128 * h + 128]

    for n in range(STEPS + 1):
        for k in range(4):
            ACC[n, k] = zero

    def early(t, _):
        acc = [zero] * 2
        for i in range(RH):
            for h in range(2):
                x = get(F, 0, PAD + i, t, h)
                acc[h] = acc[h] + x * x
        for h in range(2):
            ACC[0, h] = ACC[0, h] + acc[h]
        for n in range(1, STEPS + 1):
            acc = [zero] * 4
            for i in range(RH):
                for kind in range(2):
                    if alone(i, kind, n):
                        advance(F, n, PAD + i, t, kind, main_d(PAD + i), acc)
            for k in range(4):
                ACC[n, k] = ACC[n, k] + acc[k]
        return 0

    lax.fori_loop(0, SLOTS, early, 0)

    for k in range(16):
        halo[k].wait_recv()

    spread_main(-PAD, 0)
    spread_main(RH, RH + PAD)

    left_index = (
        jnp.clip(120 + 2 * in16, 0, 127),
        jnp.clip(121 + 2 * in16, 0, 127),
    )
    left_own = (jnp.clip(2 * in16 - 8, 0, 127), jnp.clip(2 * in16 - 7, 0, 127))
    right_own = (jnp.clip(112 + 2 * in16, 0, 127), jnp.clip(113 + 2 * in16, 0, 127))
    right_index = (jnp.clip(2 * in16 - 16, 0, 127), jnp.clip(2 * in16 - 15, 0, 127))
    for q in range(4):
        parts = [DE[8 * q : 8 * q + 8, 128 * k : 128 * k + 128] for k in range(4)]
        for h in range(2):
            x = jnp.where(
                is_left,
                jnp.where(in16 < 4, gather(parts[0], left_index[h]), gather(parts[1], left_own[h])),
                jnp.where(in16 < 8, gather(parts[2], right_own[h]), gather(parts[3], right_index[h])),
            )
            x = jnp.where(in16 < 12, x * COUPLING, 0.0)
            for i in range(8):
                row = 8 * q + i - 8 + PAD
                if 0 <= row < ROWS:
                    DB[row, :, 256 + 128 * h : 384 + 128 * h] = jnp.broadcast_to(
                        x[i : i + 1], (8, 128)
                    )

    for a in range(6):
        from_left, from_right = RC[0, a], RC[1, a]
        for b in range(4):
            row = 4 * a + b
            for h in range(2):
                if 1 <= a <= 4:
                    x = get(S, 0, row, 0, h)
                else:
                    x = own_strip([get(F, 0, row, t, h) for t in range(SLOTS)])
                spot = 4 * (2 * b + h)
                x = jnp.where(in32 < 4, roll(from_left, -spot), x)
                x = jnp.where((in32 >= 24) & (in32 < 28), roll(from_right, 24 - spot), x)
                put(S, 0, row, 0, h, x)

    def late(u, _):
        for n in range(1, STEPS + 1):
            acc = [zero] * 4
            for row in range(ROWS):
                i = row - PAD
                for kind in range(2):
                    if wanted(i, kind, n) and not (0 <= i < RH and alone(i, kind, n)):
                        for v in range(2):
                            advance(
                                F, n, row, 2 * u + v, kind, main_d(row),
                                acc if 0 <= i < RH else None,
                            )
            for k in range(4):
                ACC[n, k] = ACC[n, k] + acc[k]
        return 0

    lax.fori_loop(0, SLOTS // 2, late, 0)

    strip_acc = {}
    for n in range(1, STEPS + 1):
        acc = [zero] * 4
        for row in range(ROWS):
            i = row - PAD
            for kind in range(2):
                if wanted(i, kind, n):
                    advance(
                        S, n, row, 0, kind,
                        lambda h, row=row: DB[row, :, 256 + 128 * h : 384 + 128 * h],
                        acc if 0 <= i < RH else None,
                    )
        strip_acc[n] = acc

    base = []
    for n in range(STEPS + 1):
        for kind in range(2):
            if n == 0 and kind == 1:
                continue
            total = zero
            for h in range(2):
                x = ACC[n, 2 * kind + h]
                if n:
                    col = 2 * lane + h
                    x = jnp.where((col >= n) & (col < CH - n), x, 0.0)
                    col = jnp.where(is_left, 2 * (in16 - 4) + h, CH - 16 + 2 * in16 + h)
                    near = (col >= 0) & (col < CH) & ((is_left & (col < n)) | (~is_left & (col >= CH - n)))
                    x = x + jnp.where(near, strip_acc[n][2 * kind + h], 0.0)
                total = total + x
            q = 2 * n if kind == 0 else 2 * n - 1
            if q < 2:
                base.append(total)
            else:
                total = 2.0 * total - base[q % 2]
            SUM[q] = total
    for q in range(NQ, 24):
        SUM[q] = zero
    sums = jnp.sum(SUM[...], axis=1)
    totals = jnp.broadcast_to(jnp.sum(sums, axis=1, keepdims=True), (24, 128))
    at = lax.broadcasted_iota(jnp.int32, (24, 128), 0) == lax.broadcasted_iota(
        jnp.int32, (24, 128), 1
    )
    R1[r] = jnp.sum(jnp.where(at, totals, 0.0), axis=0, keepdims=True)

    def exchange(buf, mine, peers, send, recv):
        return [
            pltpu.make_async_remote_copy(
                src_ref=buf.at[mine], dst_ref=buf.at[mine],
                send_sem=send.at[k], recv_sem=recv.at[k],
                device_id=peer, device_id_type=MESH,
            )
            for k, peer in enumerate(peers)
        ]

    outs = [
        pltpu.make_async_copy(
            V.at[2 * k + h, sites], ref.at[:, pl.ds(128 * h, 128)], out_sem.at[k, h]
        )
        for k, ref in enumerate((prev_out, last_out))
        for h in range(2)
    ]
    weave = (lane // 2, 64 + lane // 2)
    is_even = lane % 2 == 0
    outer = (lane < 4) | (lane >= 124)

    def result(k, level):
        def one(i, _):
            strip = [get(S, level, PAD + i, 0, h) for h in range(2)]
            for t in range(SLOTS):
                index = jnp.clip(
                    jnp.where(lane < 4, 32 * t + 4 + lane, 32 * t + 20 - 124 + lane), 0, 127
                )
                x = [
                    jnp.where(outer, gather(strip[h], index), get(F, level, PAD + i, t, h))
                    for h in range(2)
                ]
                for w in range(2):
                    V.at[2 * k + w][strided(i, t), :] = jnp.where(
                        is_even, gather(x[0], weave[w]), gather(x[1], weave[w])
                    )
            return 0

        for i in range(RH):
            one(i, 0)
        for copy in outs[2 * k : 2 * k + 2]:
            copy.start()

    first = exchange(R1, r, row_peers, s1_send, s1_recv)
    for copy in first:
        copy.start()
    result(0, STEPS - 1)
    for copy in first:
        copy.wait_recv()
    mine = g * COL + c
    R2[mine] = jnp.sum(R1[...], axis=0)
    second = exchange(R2, mine, col_peers, s2_send, s2_recv)
    for copy in second:
        copy.start()
    result(1, STEPS)
    for copy in second:
        copy.wait_recv()
    mom_out[...] = jnp.sum(R2[...], axis=0) * (1.0 / COUNT)

    for copy in halo + first + second:
        copy.wait_send()
    for copy in outs:
        copy.wait()


def body(sizes, vectors, disorder):
    GR, ROW, COL = sizes
    f32 = jnp.float32
    dma = pltpu.SemaphoreType.DMA
    hbm = pl.BlockSpec(memory_space=pltpu.HBM)
    prev, last, moments = pl.pallas_call(
        functools.partial(kernel, sizes),
        out_shape=(
            jax.ShapeDtypeStruct((NV * RH, CH), f32),
            jax.ShapeDtypeStruct((NV * RH, CH), f32),
            jax.ShapeDtypeStruct((1, 128), f32),
        ),
        in_specs=[hbm, hbm],
        out_specs=(
            pl.BlockSpec(memory_space=pl.ANY),
            pl.BlockSpec(memory_space=pl.ANY),
            pl.BlockSpec(memory_space=pltpu.VMEM),
        ),
        scratch_shapes=[
            pltpu.VMEM((4, (NV + 1) * RH, 128), f32),
            pltpu.VMEM((STEPS + 1, ROWS, SLOTS, 8, CH), f32),
            pltpu.VMEM((STEPS + 1, ROWS, 1, 8, 256), f32),
            pltpu.VMEM((32, 512), f32),
            pltpu.VMEM((ROWS, 8, 512), f32),
            pltpu.VMEM((2, 4, 8, 128), f32),
            pltpu.VMEM((2, 6, 8, 128), f32),
            pltpu.VMEM((STEPS + 1, 4, 8, 128), f32),
            pltpu.VMEM((24, 8, 128), f32),
            pltpu.VMEM((ROW, 1, 128), f32),
            pltpu.VMEM((GR * COL, 1, 128), f32),
            dma((3,)),
            dma((2, 2)),
            dma((16,)),
            dma((16,)),
            dma((ROW - 1,)),
            dma((ROW - 1,)),
            dma((GR * COL - 1,)),
            dma((GR * COL - 1,)),
        ],
        compiler_params=pltpu.CompilerParams(
            collective_id=0, has_side_effects=True, vmem_limit_bytes=32 << 20
        ),
    )(
        pltpu.with_memory_space_constraint(vectors.reshape(NV * RH, CH), pltpu.HBM),
        pltpu.with_memory_space_constraint(disorder, pltpu.HBM),
    )
    return prev.reshape(vectors.shape), last.reshape(vectors.shape), moments[0, :NQ]


def solution(mesh):
    sizes = mesh.shape["grp"], mesh.shape["row"], mesh.shape["col"]
    return jax.shard_map(
        functools.partial(body, sizes),
        mesh=mesh,
        in_specs=(P("grp", "row", "col"), P("row", "col")),
        out_specs=(P("grp", "row", "col"), P("grp", "row", "col"), P()),
        check_vma=False,
    )
```

```python
import functools

import jax
import jax.numpy as jnp
from jax import lax
from jax.experimental import pallas as pl
from jax.experimental.pallas import tpu as pltpu
from jax.sharding import PartitionSpec as P

STEPS = 8
SCALE = 4.6
COUPLING = 2.0 / SCALE
MESH = pl.DeviceIdType.MESH
NQ = 2 * STEPS + 1
NV, RH, CH = 32, 16, 256
PAD = (STEPS + 1) // 2
ROWS = RH + 2 * PAD
SLOTS = NV // 8


def roll(x, shift):
    return pltpu.roll(x, shift % 128, axis=1)


def gather(x, index):
    return jnp.take_along_axis(x, index, axis=1, mode="promise_in_bounds")


def permuted(x, matrix):
    n = x.shape[0]
    parts = []
    for _ in range(3):
        parts.append(x.astype(jnp.bfloat16))
        x = x - parts[-1].astype(jnp.float32)
    y = jnp.dot(jnp.concatenate(parts, axis=0), matrix, preferred_element_type=jnp.float32)
    return y[:n] + y[n : 2 * n] + y[2 * n :]


def half_of(i, kind):
    return (i + kind) % 2


def alone(i, kind, n):
    j = RH - 1 - i
    return n <= (min(2 * i + 1, 2 * j) if kind == 0 else min(2 * i, 2 * j + 1))


def wanted(i, kind, n):
    if i < 0:
        return n <= STEPS + 1 + 2 * i - kind
    if i >= RH:
        return n <= STEPS + 1 - 2 * (i - RH + 1) - (1 - kind)
    return True


def kernel(
    sizes, vec_hbm, dis_hbm, prev_out, last_out, mom_out,
    V, F, S, DE, DB, PK, RC, ACC, SUM, R1, R2, PERM,
    load_sem, out_sem, send_sem, recv_sem, s1_send, s1_recv, s2_send, s2_recv,
):
    GR, ROW, COL = sizes
    COUNT = float(GR * NV * ROW * RH * COL * CH)
    g = lax.axis_index("grp")
    r = lax.axis_index("row")
    c = lax.axis_index("col")
    up, down = lax.rem(r + ROW - 1, ROW), lax.rem(r + 1, ROW)
    left, right = lax.rem(c + COL - 1, COL), lax.rem(c + 1, COL)

    sites = pl.ds(0, NV * RH)
    loads = [
        pltpu.make_async_copy(
            vec_hbm.at[:, pl.ds(128 * h, 128)], V.at[h, sites], load_sem.at[h]
        )
        for h in range(2)
    ]
    loads.append(
        pltpu.make_async_copy(
            dis_hbm, DE.at[pl.ds(8, RH), pl.ds(128, CH)], load_sem.at[2]
        )
    )
    for copy in loads:
        copy.start()

    row_peers = [(g, lax.rem(r + d, ROW), c) for d in sorted(range(1, ROW), key=lambda d: (-min(d, ROW - d), d))]
    col_peers = []
    for dg in range(GR):
        for dc in range(COL):
            if dg or dc:
                col_peers.append((lax.rem(g + dg, GR), r, lax.rem(c + dc, COL)))
    corners = [(g, a, b) for a in (up, down) for b in (left, right)]
    barrier = pltpu.get_barrier_semaphore()
    for peer in row_peers + col_peers + corners:
        pl.semaphore_signal(barrier, inc=1, device_id=peer, device_id_type=MESH)

    lane = lax.broadcasted_iota(jnp.int32, (8, 128), 1)
    zero = jnp.zeros((8, 128), jnp.float32)
    in16 = lane % 16
    in32 = lane % 32
    is_left = in32 < 16
    low = lane < 64
    pick = ((2 * lane) % 128, (2 * lane + 1) % 128)

    source = lax.broadcasted_iota(jnp.int32, (CH, CH), 0)
    target = lax.broadcasted_iota(jnp.int32, (CH, CH), 1)
    half = CH // 2
    to_halves = jnp.where(target < half, 2 * target, 2 * target - CH + 1) == source
    to_columns = jnp.where(source < half, 2 * source, 2 * source - CH + 1) == target
    for k, pick_one in enumerate((to_halves, to_columns)):
        PERM[k] = jnp.where(pick_one, 1.0, 0.0).astype(jnp.bfloat16)

    for copy in loads:
        copy.wait()

    def strided(i, t):
        return pl.ds(t * 8 * RH + i, 8, stride=RH)

    def split(m0, m1):
        return [jnp.where(low, gather(m0, p), gather(m1, p)) for p in pick]

    def get(ref, n, row, t, h):
        return ref[n, row, t, :, 128 * h : 128 * h + 128]

    def put(ref, n, row, t, h, x):
        ref[n, row, t, :, 128 * h : 128 * h + 128] = x

    strip_index = jnp.where(
        is_left, jnp.clip(in16 - 4, 0, 127), jnp.clip(120 + in16, 0, 127)
    )
    strip_own = (is_left & (in16 >= 4) & (in16 < 12)) | (~is_left & (in16 < 8))

    def own_strip(parts):
        x = gather(parts[0], strip_index)
        for t in range(1, SLOTS):
            x = jnp.where(lane >= 32 * t, gather(parts[t], strip_index), x)
        return jnp.where(strip_own, x, 0.0)

    chunk = 64

    def to_parity(k, _):
        at = pl.ds(pl.multiple_of(chunk * k, chunk), chunk)
        y = permuted(jnp.concatenate([V[0, at, :], V[1, at, :]], axis=1), PERM[0])
        V[2, at, :] = y[:, :128]
        V[3, at, :] = y[:, 128:]
        return 0

    lax.fori_loop(0, NV * RH // chunk, to_parity, 0)

    order = [0, 1, 2, 3, 12, 13, 14, 15] + list(range(4, 12))
    packed = {}
    for i in order:
        parts = ([], [])
        for t in range(SLOTS):
            for h in range(2):
                x = V.at[2 + h][strided(i, t), :]
                put(F, 0, PAD + i, t, h, x)
                parts[h].append(x)
        for h in range(2):
            x = own_strip(parts[h])
            put(S, 0, PAD + i, 0, h, x)
            a, spot = i // 4, 4 * (2 * (i % 4) + h)
            m = (in32 >= spot) & (in32 < spot + 4)
            for side, edge in ((0, 4), (1, 20)):
                packed[side, a] = jnp.where(m, roll(x, spot - edge), packed.get((side, a), zero))
                if i % 4 == 3 and h == 1:
                    PK[side, a] = packed[side, a]

    pl.semaphore_wait(barrier, len(row_peers) + len(col_peers) + len(corners))

    mid = pl.ds(128, CH)
    plan = [
        (F.at[0, pl.ds(PAD + RH - PAD, PAD)], F.at[0, pl.ds(0, PAD)], (g, down, c)),
        (F.at[0, pl.ds(PAD, PAD)], F.at[0, pl.ds(PAD + RH, PAD)], (g, up, c)),
        (PK.at[1], RC.at[0, pl.ds(1, 4)], (g, r, right)),
        (PK.at[0], RC.at[1, pl.ds(1, 4)], (g, r, left)),
        (PK.at[1, 3], RC.at[0, 0], (g, down, right)),
        (PK.at[1, 0], RC.at[0, 5], (g, up, right)),
        (PK.at[0, 3], RC.at[1, 0], (g, down, left)),
        (PK.at[0, 0], RC.at[1, 5], (g, up, left)),
        (DE.at[pl.ds(16, 8), mid], DE.at[pl.ds(0, 8), mid], (g, down, c)),
        (DE.at[pl.ds(8, 8), mid], DE.at[pl.ds(24, 8), mid], (g, up, c)),
        (DE.at[pl.ds(8, 16), pl.ds(256, 128)], DE.at[pl.ds(8, 16), pl.ds(0, 128)], (g, r, right)),
        (DE.at[pl.ds(8, 16), pl.ds(128, 128)], DE.at[pl.ds(8, 16), pl.ds(384, 128)], (g, r, left)),
        (DE.at[pl.ds(16, 8), pl.ds(256, 128)], DE.at[pl.ds(0, 8), pl.ds(0, 128)], (g, down, right)),
        (DE.at[pl.ds(8, 8), pl.ds(256, 128)], DE.at[pl.ds(24, 8), pl.ds(0, 128)], (g, up, right)),
        (DE.at[pl.ds(16, 8), pl.ds(128, 128)], DE.at[pl.ds(0, 8), pl.ds(384, 128)], (g, down, left)),
        (DE.at[pl.ds(8, 8), pl.ds(128, 128)], DE.at[pl.ds(24, 8), pl.ds(384, 128)], (g, up, left)),
    ]
    halo = [
        pltpu.make_async_remote_copy(
            src_ref=source, dst_ref=target, send_sem=send_sem.at[k], recv_sem=recv_sem.at[k],
            device_id=device, device_id_type=MESH,
        )
        for k, (source, target, device) in enumerate(plan)
    ]
    for k in [4, 5, 6, 7, 2, 3, 12, 13, 14, 15, 10, 11, 0, 1, 8, 9]:
        halo[k].start()

    def spread_main(lo, hi):
        for q in range(4):
            rows = [i for i in range(8) if lo <= 8 * q + i - 8 < hi]
            if rows:
                x = split(DE[8 * q : 8 * q + 8, 128:256], DE[8 * q : 8 * q + 8, 256:384])
                for h in range(2):
                    y = x[h] * COUPLING
                    for i in rows:
                        DB[8 * q + i - 8 + PAD, :, 128 * h : 128 * h + 128] = jnp.broadcast_to(
                            y[i : i + 1], (8, 128)
                        )

    spread_main(0, RH)

    def advance(ref, n, row, t, kind, d, acc):
        h = half_of(row, kind)
        centre = get(ref, n - 1, row, t, h)
        other = get(ref, n - 1, row, t, 1 - h)
        bond = get(ref, n - 1, row + 1 - 2 * kind, t, h)
        around = other + roll(other, 1 if h == 0 else -1) + bond
        new = d(h) * centre - COUPLING * around
        new = 0.5 * new if n == 1 else new - get(ref, n - 2, row, t, h)
        put(ref, n, row, t, h, new)
        if acc is not None:
            acc[h] = acc[h] + new * new
            acc[2 + h] = acc[2 + h] + new * centre

    def main_d(row):
        return lambda h: DB[row, :, 128 * h : 128 * h + 128]

    for n in range(STEPS + 1):
        for k in range(4):
            ACC[n, k] = zero

    def early(t, _):
        acc = [zero] * 2
        for i in range(RH):
            for h in range(2):
                x = get(F, 0, PAD + i, t, h)
                acc[h] = acc[h] + x * x
        for h in range(2):
            ACC[0, h] = ACC[0, h] + acc[h]
        for n in range(1, STEPS + 1):
            acc = [zero] * 4
            for i in range(RH):
                for kind in range(2):
                    if alone(i, kind, n):
                        advance(F, n, PAD + i, t, kind, main_d(PAD + i), acc)
            for k in range(4):
                ACC[n, k] = ACC[n, k] + acc[k]
        return 0

    lax.fori_loop(0, SLOTS, early, 0)

    by_row = [0, 1, 8, 9]
    for k in by_row:
        halo[k].wait_recv()

    spread_main(-PAD, 0)
    spread_main(RH, RH + PAD)

    def late(u, _):
        for n in range(1, STEPS + 1):
            acc = [zero] * 4
            for row in range(ROWS):
                i = row - PAD
                for kind in range(2):
                    if wanted(i, kind, n) and not (0 <= i < RH and alone(i, kind, n)):
                        for v in range(2):
                            advance(
                                F, n, row, 2 * u + v, kind, main_d(row),
                                acc if 0 <= i < RH else None,
                            )
            for k in range(4):
                ACC[n, k] = ACC[n, k] + acc[k]
        return 0

    lax.fori_loop(0, SLOTS // 2, late, 0)

    for k in range(16):
        if k not in by_row:
            halo[k].wait_recv()

    left_index = (
        jnp.clip(120 + 2 * in16, 0, 127),
        jnp.clip(121 + 2 * in16, 0, 127),
    )
    left_own = (jnp.clip(2 * in16 - 8, 0, 127), jnp.clip(2 * in16 - 7, 0, 127))
    right_own = (jnp.clip(112 + 2 * in16, 0, 127), jnp.clip(113 + 2 * in16, 0, 127))
    right_index = (jnp.clip(2 * in16 - 16, 0, 127), jnp.clip(2 * in16 - 15, 0, 127))
    for q in range(4):
        parts = [DE[8 * q : 8 * q + 8, 128 * k : 128 * k + 128] for k in range(4)]
        for h in range(2):
            x = jnp.where(
                is_left,
                jnp.where(in16 < 4, gather(parts[0], left_index[h]), gather(parts[1], left_own[h])),
                jnp.where(in16 < 8, gather(parts[2], right_own[h]), gather(parts[3], right_index[h])),
            )
            x = jnp.where(in16 < 12, x * COUPLING, 0.0)
            for i in range(8):
                row = 8 * q + i - 8 + PAD
                if 0 <= row < ROWS:
                    DB[row, :, 256 + 128 * h : 384 + 128 * h] = jnp.broadcast_to(
                        x[i : i + 1], (8, 128)
                    )

    for a in range(6):
        from_left, from_right = RC[0, a], RC[1, a]
        for b in range(4):
            row = 4 * a + b
            for h in range(2):
                if 1 <= a <= 4:
                    x = get(S, 0, row, 0, h)
                else:
                    x = own_strip([get(F, 0, row, t, h) for t in range(SLOTS)])
                spot = 4 * (2 * b + h)
                x = jnp.where(in32 < 4, roll(from_left, -spot), x)
                x = jnp.where((in32 >= 24) & (in32 < 28), roll(from_right, 24 - spot), x)
                put(S, 0, row, 0, h, x)

    strip_acc = {}
    for n in range(1, STEPS + 1):
        acc = [zero] * 4
        for row in range(ROWS):
            i = row - PAD
            for kind in range(2):
                if wanted(i, kind, n):
                    advance(
                        S, n, row, 0, kind,
                        lambda h, row=row: DB[row, :, 256 + 128 * h : 384 + 128 * h],
                        acc if 0 <= i < RH else None,
                    )
        strip_acc[n] = acc

    base = []
    for n in range(STEPS + 1):
        for kind in range(2):
            if n == 0 and kind == 1:
                continue
            total = zero
            for h in range(2):
                x = ACC[n, 2 * kind + h]
                if n:
                    col = 2 * lane + h
                    x = jnp.where((col >= n) & (col < CH - n), x, 0.0)
                    col = jnp.where(is_left, 2 * (in16 - 4) + h, CH - 16 + 2 * in16 + h)
                    near = (col >= 0) & (col < CH) & ((is_left & (col < n)) | (~is_left & (col >= CH - n)))
                    x = x + jnp.where(near, strip_acc[n][2 * kind + h], 0.0)
                total = total + x
            q = 2 * n if kind == 0 else 2 * n - 1
            if q < 2:
                base.append(total)
            else:
                total = 2.0 * total - base[q % 2]
            SUM[q] = total
    for q in range(NQ, 24):
        SUM[q] = zero
    sums = jnp.sum(SUM[...], axis=1)
    totals = jnp.broadcast_to(jnp.sum(sums, axis=1, keepdims=True), (24, 128))
    at = lax.broadcasted_iota(jnp.int32, (24, 128), 0) == lax.broadcasted_iota(
        jnp.int32, (24, 128), 1
    )
    R1[r] = jnp.sum(jnp.where(at, totals, 0.0), axis=0, keepdims=True)

    def exchange(buf, mine, peers, send, recv):
        return [
            pltpu.make_async_remote_copy(
                src_ref=buf.at[mine], dst_ref=buf.at[mine],
                send_sem=send.at[k], recv_sem=recv.at[k],
                device_id=peer, device_id_type=MESH,
            )
            for k, peer in enumerate(peers)
        ]

    outs = [
        pltpu.make_async_copy(
            V.at[2 * k + h, sites], ref.at[:, pl.ds(128 * h, 128)], out_sem.at[k, h]
        )
        for k, ref in enumerate((prev_out, last_out))
        for h in range(2)
    ]
    outer = (lane < 4) | (lane >= 124)

    def result(k, level):
        def four(a, _):
            rows = []
            for b in range(4):
                row = PAD + 4 * a + b
                strip = [get(S, level, row, 0, h) for h in range(2)]
                for t in range(SLOTS):
                    index = jnp.clip(
                        jnp.where(lane < 4, 32 * t + 4 + lane, 32 * t + 20 - 124 + lane), 0, 127
                    )
                    x = [
                        jnp.where(outer, gather(strip[h], index), get(F, level, row, t, h))
                        for h in range(2)
                    ]
                    rows.append(jnp.concatenate(x, axis=1))
            y = permuted(jnp.concatenate(rows, axis=0), PERM[1])
            for b in range(4):
                for t in range(SLOTS):
                    at = NV * b + 8 * t
                    for w in range(2):
                        V.at[2 * k + w][strided(4 * a + b, t), :] = y[
                            at : at + 8, 128 * w : 128 * w + 128
                        ]
            return 0

        lax.fori_loop(0, RH // 4, four, 0)
        for copy in outs[2 * k : 2 * k + 2]:
            copy.start()

    first = exchange(R1, r, row_peers, s1_send, s1_recv)
    for copy in first:
        copy.start()
    result(0, STEPS - 1)
    for copy in halo:
        copy.wait_send()
    for copy in first:
        copy.wait_recv()
    mine = g * COL + c
    R2[mine] = jnp.sum(R1[...], axis=0)
    second = exchange(R2, mine, col_peers, s2_send, s2_recv)
    for copy in second:
        copy.start()
    result(1, STEPS)
    for copy in first:
        copy.wait_send()
    for copy in second:
        copy.wait_recv()
    mom_out[...] = jnp.sum(R2[...], axis=0) * (1.0 / COUNT)

    for copy in second:
        copy.wait_send()
    for copy in outs:
        copy.wait()


def store(prev, last, sums, prev_out, last_out, mom_out, row, sem):
    copies = [
        pltpu.make_async_copy(prev, prev_out, sem.at[0]),
        pltpu.make_async_copy(last, last_out, sem.at[1]),
    ]
    for copy in copies:
        copy.start()
    row[...] = sums[0, :NQ]
    copies.append(pltpu.make_async_copy(row, mom_out, sem.at[2]))
    copies[2].start()
    for copy in copies:
        copy.wait()


def body(sizes, vectors, disorder):
    GR, ROW, COL = sizes
    f32 = jnp.float32
    dma = pltpu.SemaphoreType.DMA
    hbm = pl.BlockSpec(memory_space=pltpu.HBM)
    prev, last, moments = pl.pallas_call(
        functools.partial(kernel, sizes),
        out_shape=(
            jax.ShapeDtypeStruct((NV * RH, CH), f32),
            jax.ShapeDtypeStruct((NV * RH, CH), f32),
            jax.ShapeDtypeStruct((1, 128), f32),
        ),
        in_specs=[hbm, hbm],
        out_specs=(
            pl.BlockSpec(memory_space=pl.ANY),
            pl.BlockSpec(memory_space=pl.ANY),
            pl.BlockSpec(memory_space=pltpu.VMEM),
        ),
        scratch_shapes=[
            pltpu.VMEM((4, (NV + 1) * RH, 128), f32),
            pltpu.VMEM((STEPS + 1, ROWS, SLOTS, 8, CH), f32),
            pltpu.VMEM((STEPS + 1, ROWS, 1, 8, 256), f32),
            pltpu.VMEM((32, 512), f32),
            pltpu.VMEM((ROWS, 8, 512), f32),
            pltpu.VMEM((2, 4, 8, 128), f32),
            pltpu.VMEM((2, 6, 8, 128), f32),
            pltpu.VMEM((STEPS + 1, 4, 8, 128), f32),
            pltpu.VMEM((24, 8, 128), f32),
            pltpu.VMEM((ROW, 1, 128), f32),
            pltpu.VMEM((GR * COL, 1, 128), f32),
            pltpu.VMEM((2, CH, CH), jnp.bfloat16),
            dma((3,)),
            dma((2, 2)),
            dma((16,)),
            dma((16,)),
            dma((ROW - 1,)),
            dma((ROW - 1,)),
            dma((GR * COL - 1,)),
            dma((GR * COL - 1,)),
        ],
        compiler_params=pltpu.CompilerParams(
            collective_id=0, has_side_effects=True, vmem_limit_bytes=32 << 20
        ),
    )(
        pltpu.with_memory_space_constraint(vectors.reshape(NV * RH, CH), pltpu.HBM),
        pltpu.with_memory_space_constraint(disorder, pltpu.HBM),
    )
    anywhere = pl.BlockSpec(memory_space=pl.ANY)
    prev, last, moments = pl.pallas_call(
        store,
        out_shape=(
            jax.ShapeDtypeStruct((NV * RH, CH), f32),
            jax.ShapeDtypeStruct((NV * RH, CH), f32),
            jax.ShapeDtypeStruct((NQ,), f32),
        ),
        in_specs=[anywhere, anywhere, pl.BlockSpec(memory_space=pltpu.VMEM)],
        out_specs=(anywhere, anywhere, anywhere),
        scratch_shapes=[pltpu.VMEM((NQ,), f32), dma((3,))],
        compiler_params=pltpu.CompilerParams(vmem_limit_bytes=1 << 20),
    )(prev, last, moments)
    return prev.reshape(vectors.shape), last.reshape(vectors.shape), moments


def solution(mesh):
    sizes = mesh.shape["grp"], mesh.shape["row"], mesh.shape["col"]
    return jax.shard_map(
        functools.partial(body, sizes),
        mesh=mesh,
        in_specs=(P("grp", "row", "col"), P("row", "col")),
        out_specs=(P("grp", "row", "col"), P("grp", "row", "col"), P()),
        check_vma=False,
    )
```

```python
import functools

import jax
import jax.numpy as jnp
from jax import lax
from jax.experimental import pallas as pl
from jax.experimental.pallas import tpu as pltpu
from jax.sharding import PartitionSpec as P

STEPS = 8
SCALE = 4.6
COUPLING = 2.0 / SCALE
MESH = pl.DeviceIdType.MESH
NQ = 2 * STEPS + 1
NV, RH, CH = 32, 16, 256
PAD = (STEPS + 1) // 2
ROWS = RH + 2 * PAD
SLOTS = NV // 8


def roll(x, shift):
    return pltpu.roll(x, shift % 128, axis=1)


def gather(x, index):
    return jnp.take_along_axis(x, index, axis=1, mode="promise_in_bounds")


def permuted(x, matrix):
    n = x.shape[0]
    parts = []
    for _ in range(3):
        parts.append(x.astype(jnp.bfloat16))
        x = x - parts[-1].astype(jnp.float32)
    y = jnp.dot(jnp.concatenate(parts, axis=0), matrix, preferred_element_type=jnp.float32)
    return y[:n] + y[n : 2 * n] + y[2 * n :]


def half_of(i, kind):
    return (i + kind) % 2


def alone(i, kind, n):
    j = RH - 1 - i
    return n <= (min(2 * i + 1, 2 * j) if kind == 0 else min(2 * i, 2 * j + 1))


def wanted(i, kind, n):
    if i < 0:
        return n <= STEPS + 1 + 2 * i - kind
    if i >= RH:
        return n <= STEPS + 1 - 2 * (i - RH + 1) - (1 - kind)
    return True


def kernel(
    sizes, vec_hbm, dis_hbm, prev_out, last_out, mom_out,
    V, F, S, DE, DB, PK, RC, ACC, SUM, R1, R2, PERM,
    load_sem, out_sem, send_sem, recv_sem, s1_send, s1_recv, s2_send, s2_recv,
):
    GR, ROW, COL = sizes
    COUNT = float(GR * NV * ROW * RH * COL * CH)
    g = lax.axis_index("grp")
    r = lax.axis_index("row")
    c = lax.axis_index("col")
    up, down = lax.rem(r + ROW - 1, ROW), lax.rem(r + 1, ROW)
    left, right = lax.rem(c + COL - 1, COL), lax.rem(c + 1, COL)

    sites = pl.ds(0, NV * RH)
    loads = [
        pltpu.make_async_copy(
            vec_hbm.at[:, pl.ds(128 * h, 128)], V.at[h, sites], load_sem.at[h]
        )
        for h in range(2)
    ]
    loads.append(
        pltpu.make_async_copy(
            dis_hbm, DE.at[pl.ds(8, RH), pl.ds(128, CH)], load_sem.at[2]
        )
    )
    for copy in loads:
        copy.start()

    row_peers = [(g, lax.rem(r + d, ROW), c) for d in sorted(range(1, ROW), key=lambda d: (-min(d, ROW - d), d))]
    col_peers = []
    for dg in reversed(range(GR)):
        for dc in sorted(range(COL), key=lambda d: (-min(d, COL - d), d)):
            if dg or dc:
                col_peers.append((lax.rem(g + dg, GR), r, lax.rem(c + dc, COL)))
    corners = [(g, a, b) for a in (up, down) for b in (left, right)]
    barrier = pltpu.get_barrier_semaphore()
    for peer in row_peers + col_peers + corners:
        pl.semaphore_signal(barrier, inc=1, device_id=peer, device_id_type=MESH)

    lane = lax.broadcasted_iota(jnp.int32, (8, 128), 1)
    zero = jnp.zeros((8, 128), jnp.float32)
    in16 = lane % 16
    in32 = lane % 32
    is_left = in32 < 16
    low = lane < 64
    pick = ((2 * lane) % 128, (2 * lane + 1) % 128)

    source = lax.broadcasted_iota(jnp.int32, (CH, CH), 0)
    target = lax.broadcasted_iota(jnp.int32, (CH, CH), 1)
    half = CH // 2
    to_halves = jnp.where(target < half, 2 * target, 2 * target - CH + 1) == source
    to_columns = jnp.where(source < half, 2 * source, 2 * source - CH + 1) == target
    for k, pick_one in enumerate((to_halves, to_columns)):
        PERM[k] = jnp.where(pick_one, 1.0, 0.0).astype(jnp.bfloat16)

    for copy in loads:
        copy.wait()

    def strided(i, t):
        return pl.ds(t * 8 * RH + i, 8, stride=RH)

    def split(m0, m1):
        return [jnp.where(low, gather(m0, p), gather(m1, p)) for p in pick]

    def get(ref, n, row, t, h):
        return ref[n, row, t, :, 128 * h : 128 * h + 128]

    def put(ref, n, row, t, h, x):
        ref[n, row, t, :, 128 * h : 128 * h + 128] = x

    strip_index = jnp.where(
        is_left, jnp.clip(in16 - 4, 0, 127), jnp.clip(120 + in16, 0, 127)
    )
    strip_own = (is_left & (in16 >= 4) & (in16 < 12)) | (~is_left & (in16 < 8))

    def own_strip(parts):
        x = gather(parts[0], strip_index)
        for t in range(1, SLOTS):
            x = jnp.where(lane >= 32 * t, gather(parts[t], strip_index), x)
        return jnp.where(strip_own, x, 0.0)

    chunk = 128

    def to_parity(k, _):
        at = pl.ds(pl.multiple_of(chunk * k, chunk), chunk)
        y = permuted(jnp.concatenate([V[0, at, :], V[1, at, :]], axis=1), PERM[0])
        V[2, at, :] = y[:, :128]
        V[3, at, :] = y[:, 128:]
        return 0

    lax.fori_loop(0, NV * RH // chunk, to_parity, 0)

    order = [0, 1, 2, 3, 12, 13, 14, 15] + list(range(4, 12))
    for i in order:
        for t in range(SLOTS):
            for h in range(2):
                put(F, 0, PAD + i, t, h, V.at[2 + h][strided(i, t), :])

    pl.semaphore_wait(barrier, len(row_peers) + len(col_peers) + len(corners))

    mid = pl.ds(128, CH)
    plan = [
        (F.at[0, pl.ds(PAD + RH - PAD, PAD)], F.at[0, pl.ds(0, PAD)], (g, down, c)),
        (F.at[0, pl.ds(PAD, PAD)], F.at[0, pl.ds(PAD + RH, PAD)], (g, up, c)),
        (PK.at[1], RC.at[0, pl.ds(1, 4)], (g, r, right)),
        (PK.at[0], RC.at[1, pl.ds(1, 4)], (g, r, left)),
        (PK.at[1, 3], RC.at[0, 0], (g, down, right)),
        (PK.at[1, 0], RC.at[0, 5], (g, up, right)),
        (PK.at[0, 3], RC.at[1, 0], (g, down, left)),
        (PK.at[0, 0], RC.at[1, 5], (g, up, left)),
        (DE.at[pl.ds(16, 8), mid], DE.at[pl.ds(0, 8), mid], (g, down, c)),
        (DE.at[pl.ds(8, 8), mid], DE.at[pl.ds(24, 8), mid], (g, up, c)),
        (DE.at[pl.ds(8, 16), pl.ds(256, 128)], DE.at[pl.ds(8, 16), pl.ds(0, 128)], (g, r, right)),
        (DE.at[pl.ds(8, 16), pl.ds(128, 128)], DE.at[pl.ds(8, 16), pl.ds(384, 128)], (g, r, left)),
        (DE.at[pl.ds(16, 8), pl.ds(256, 128)], DE.at[pl.ds(0, 8), pl.ds(0, 128)], (g, down, right)),
        (DE.at[pl.ds(8, 8), pl.ds(256, 128)], DE.at[pl.ds(24, 8), pl.ds(0, 128)], (g, up, right)),
        (DE.at[pl.ds(16, 8), pl.ds(128, 128)], DE.at[pl.ds(0, 8), pl.ds(384, 128)], (g, down, left)),
        (DE.at[pl.ds(8, 8), pl.ds(128, 128)], DE.at[pl.ds(24, 8), pl.ds(384, 128)], (g, up, left)),
    ]
    halo = [
        pltpu.make_async_remote_copy(
            src_ref=source, dst_ref=target, send_sem=send_sem.at[k], recv_sem=recv_sem.at[k],
            device_id=device, device_id_type=MESH,
        )
        for k, (source, target, device) in enumerate(plan)
    ]
    for k in [0, 1, 8, 9]:
        halo[k].start()

    packed = {}
    for i in order:
        for h in range(2):
            x = own_strip([get(F, 0, PAD + i, t, h) for t in range(SLOTS)])
            put(S, 0, PAD + i, 0, h, x)
            a, spot = i // 4, 4 * (2 * (i % 4) + h)
            m = (in32 >= spot) & (in32 < spot + 4)
            for side, edge in ((0, 4), (1, 20)):
                packed[side, a] = jnp.where(m, roll(x, spot - edge), packed.get((side, a), zero))
                if i % 4 == 3 and h == 1:
                    PK[side, a] = packed[side, a]

    for k in [4, 5, 6, 7, 2, 3, 12, 13, 14, 15, 10, 11]:
        halo[k].start()

    def spread_main(lo, hi):
        for q in range(4):
            rows = [i for i in range(8) if lo <= 8 * q + i - 8 < hi]
            if rows:
                x = split(DE[8 * q : 8 * q + 8, 128:256], DE[8 * q : 8 * q + 8, 256:384])
                for h in range(2):
                    y = x[h] * COUPLING
                    for i in rows:
                        DB[8 * q + i - 8 + PAD, :, 128 * h : 128 * h + 128] = jnp.broadcast_to(
                            y[i : i + 1], (8, 128)
                        )

    spread_main(0, RH)

    def advance(ref, n, row, t, kind, d, acc):
        h = half_of(row, kind)
        centre = get(ref, n - 1, row, t, h)
        other = get(ref, n - 1, row, t, 1 - h)
        bond = get(ref, n - 1, row + 1 - 2 * kind, t, h)
        around = other + roll(other, 1 if h == 0 else -1) + bond
        new = d(h) * centre - COUPLING * around
        new = 0.5 * new if n == 1 else new - get(ref, n - 2, row, t, h)
        put(ref, n, row, t, h, new)
        if acc is not None:
            acc[h] = acc[h] + new * new
            acc[2 + h] = acc[2 + h] + new * centre

    def main_d(row):
        return lambda h: DB[row, :, 128 * h : 128 * h + 128]

    for n in range(STEPS + 1):
        for k in range(4):
            ACC[n, k] = zero

    def early(u, _):
        acc = [zero] * 2
        for i in range(RH):
            for v in range(2):
                for h in range(2):
                    x = get(F, 0, PAD + i, 2 * u + v, h)
                    acc[h] = acc[h] + x * x
        for h in range(2):
            ACC[0, h] = ACC[0, h] + acc[h]
        for n in range(1, STEPS + 1):
            acc = [zero] * 4
            for i in range(RH):
                for kind in range(2):
                    if alone(i, kind, n):
                        for v in range(2):
                            advance(F, n, PAD + i, 2 * u + v, kind, main_d(PAD + i), acc)
            for k in range(4):
                ACC[n, k] = ACC[n, k] + acc[k]
        return 0

    lax.fori_loop(0, SLOTS // 2, early, 0)

    by_row = [0, 1, 8, 9]
    for k in by_row:
        halo[k].wait_recv()

    spread_main(-PAD, 0)
    spread_main(RH, RH + PAD)

    def late(u, _):
        for n in range(1, STEPS + 1):
            acc = [zero] * 4
            for row in range(ROWS):
                i = row - PAD
                for kind in range(2):
                    if wanted(i, kind, n) and not (0 <= i < RH and alone(i, kind, n)):
                        for v in range(2):
                            advance(
                                F, n, row, 2 * u + v, kind, main_d(row),
                                acc if 0 <= i < RH else None,
                            )
            for k in range(4):
                ACC[n, k] = ACC[n, k] + acc[k]
        return 0

    lax.fori_loop(0, SLOTS // 2, late, 0)

    for row in [*range(PAD), *range(PAD + RH, ROWS)]:
        for h in range(2):
            put(S, 0, row, 0, h, own_strip([get(F, 0, row, t, h) for t in range(SLOTS)]))

    for k in range(16):
        if k not in by_row:
            halo[k].wait_recv()

    left_index = (
        jnp.clip(120 + 2 * in16, 0, 127),
        jnp.clip(121 + 2 * in16, 0, 127),
    )
    left_own = (jnp.clip(2 * in16 - 8, 0, 127), jnp.clip(2 * in16 - 7, 0, 127))
    right_own = (jnp.clip(112 + 2 * in16, 0, 127), jnp.clip(113 + 2 * in16, 0, 127))
    right_index = (jnp.clip(2 * in16 - 16, 0, 127), jnp.clip(2 * in16 - 15, 0, 127))
    for q in range(4):
        parts = [DE[8 * q : 8 * q + 8, 128 * k : 128 * k + 128] for k in range(4)]
        for h in range(2):
            x = jnp.where(
                is_left,
                jnp.where(in16 < 4, gather(parts[0], left_index[h]), gather(parts[1], left_own[h])),
                jnp.where(in16 < 8, gather(parts[2], right_own[h]), gather(parts[3], right_index[h])),
            )
            x = jnp.where(in16 < 12, x * COUPLING, 0.0)
            for i in range(8):
                row = 8 * q + i - 8 + PAD
                if 0 <= row < ROWS:
                    DB[row, :, 256 + 128 * h : 384 + 128 * h] = jnp.broadcast_to(
                        x[i : i + 1], (8, 128)
                    )

    for a in range(6):
        from_left, from_right = RC[0, a], RC[1, a]
        for b in range(4):
            row = 4 * a + b
            for h in range(2):
                x = get(S, 0, row, 0, h)
                spot = 4 * (2 * b + h)
                x = jnp.where(in32 < 4, roll(from_left, -spot), x)
                x = jnp.where((in32 >= 24) & (in32 < 28), roll(from_right, 24 - spot), x)
                put(S, 0, row, 0, h, x)

    strip_acc = {}
    for n in range(1, STEPS + 1):
        acc = [zero] * 4
        for row in range(ROWS):
            i = row - PAD
            for kind in range(2):
                if wanted(i, kind, n):
                    advance(
                        S, n, row, 0, kind,
                        lambda h, row=row: DB[row, :, 256 + 128 * h : 384 + 128 * h],
                        acc if 0 <= i < RH else None,
                    )
        strip_acc[n] = acc

    base = []
    for n in range(STEPS + 1):
        for kind in range(2):
            if n == 0 and kind == 1:
                continue
            total = zero
            for h in range(2):
                x = ACC[n, 2 * kind + h]
                if n:
                    col = 2 * lane + h
                    x = jnp.where((col >= n) & (col < CH - n), x, 0.0)
                    col = jnp.where(is_left, 2 * (in16 - 4) + h, CH - 16 + 2 * in16 + h)
                    near = (col >= 0) & (col < CH) & ((is_left & (col < n)) | (~is_left & (col >= CH - n)))
                    x = x + jnp.where(near, strip_acc[n][2 * kind + h], 0.0)
                total = total + x
            q = 2 * n if kind == 0 else 2 * n - 1
            if q < 2:
                base.append(total)
            else:
                total = 2.0 * total - base[q % 2]
            SUM[q] = total
    for q in range(NQ, 24):
        SUM[q] = zero
    sums = jnp.sum(SUM[...], axis=1)
    totals = jnp.broadcast_to(jnp.sum(sums, axis=1, keepdims=True), (24, 128))
    at = lax.broadcasted_iota(jnp.int32, (24, 128), 0) == lax.broadcasted_iota(
        jnp.int32, (24, 128), 1
    )
    R1[r] = jnp.sum(jnp.where(at, totals, 0.0), axis=0, keepdims=True)

    def exchange(buf, mine, peers, send, recv):
        return [
            pltpu.make_async_remote_copy(
                src_ref=buf.at[mine], dst_ref=buf.at[mine],
                send_sem=send.at[k], recv_sem=recv.at[k],
                device_id=peer, device_id_type=MESH,
            )
            for k, peer in enumerate(peers)
        ]

    outs = [
        pltpu.make_async_copy(
            V.at[2 * k + h, sites], ref.at[:, pl.ds(128 * h, 128)], out_sem.at[k, h]
        )
        for k, ref in enumerate((prev_out, last_out))
        for h in range(2)
    ]
    outer = (lane < 4) | (lane >= 124)

    def result(k, level):
        def four(a, _):
            rows = []
            for b in range(4):
                row = PAD + 4 * a + b
                strip = [get(S, level, row, 0, h) for h in range(2)]
                for t in range(SLOTS):
                    index = jnp.clip(
                        jnp.where(lane < 4, 32 * t + 4 + lane, 32 * t + 20 - 124 + lane), 0, 127
                    )
                    x = [
                        jnp.where(outer, gather(strip[h], index), get(F, level, row, t, h))
                        for h in range(2)
                    ]
                    rows.append(jnp.concatenate(x, axis=1))
            y = permuted(jnp.concatenate(rows, axis=0), PERM[1])
            for b in range(4):
                for t in range(SLOTS):
                    at = NV * b + 8 * t
                    for w in range(2):
                        V.at[2 * k + w][strided(4 * a + b, t), :] = y[
                            at : at + 8, 128 * w : 128 * w + 128
                        ]
            return 0

        lax.fori_loop(0, RH // 4, four, 0)
        for copy in outs[2 * k : 2 * k + 2]:
            copy.start()

    first = exchange(R1, r, row_peers, s1_send, s1_recv)
    for copy in first:
        copy.start()
    result(0, STEPS - 1)
    for copy in halo:
        copy.wait_send()
    for copy in first:
        copy.wait_recv()
    mine = g * COL + c
    R2[mine] = jnp.sum(R1[...], axis=0)
    second = exchange(R2, mine, col_peers, s2_send, s2_recv)
    for copy in second:
        copy.start()
    result(1, STEPS)
    for copy in first:
        copy.wait_send()
    for copy in second:
        copy.wait_recv()
    mom_out[...] = jnp.sum(R2[...], axis=0) * (1.0 / COUNT)

    for copy in second:
        copy.wait_send()
    for copy in outs:
        copy.wait()


def store(prev, last, sums, prev_out, last_out, mom_out, row, sem):
    copies = [
        pltpu.make_async_copy(prev, prev_out, sem.at[0]),
        pltpu.make_async_copy(last, last_out, sem.at[1]),
    ]
    for copy in copies:
        copy.start()
    row[...] = sums[0, :NQ]
    copies.append(pltpu.make_async_copy(row, mom_out, sem.at[2]))
    copies[2].start()
    for copy in copies:
        copy.wait()


def body(sizes, vectors, disorder):
    GR, ROW, COL = sizes
    f32 = jnp.float32
    dma = pltpu.SemaphoreType.DMA
    hbm = pl.BlockSpec(memory_space=pltpu.HBM)
    prev, last, moments = pl.pallas_call(
        functools.partial(kernel, sizes),
        out_shape=(
            jax.ShapeDtypeStruct((NV * RH, CH), f32),
            jax.ShapeDtypeStruct((NV * RH, CH), f32),
            jax.ShapeDtypeStruct((1, 128), f32),
        ),
        in_specs=[hbm, hbm],
        out_specs=(
            pl.BlockSpec(memory_space=pl.ANY),
            pl.BlockSpec(memory_space=pl.ANY),
            pl.BlockSpec(memory_space=pltpu.VMEM),
        ),
        scratch_shapes=[
            pltpu.VMEM((4, (NV + 1) * RH, 128), f32),
            pltpu.VMEM((STEPS + 1, ROWS, SLOTS, 8, CH), f32),
            pltpu.VMEM((STEPS + 1, ROWS, 1, 8, 256), f32),
            pltpu.VMEM((32, 512), f32),
            pltpu.VMEM((ROWS, 8, 512), f32),
            pltpu.VMEM((2, 4, 8, 128), f32),
            pltpu.VMEM((2, 6, 8, 128), f32),
            pltpu.VMEM((STEPS + 1, 4, 8, 128), f32),
            pltpu.VMEM((24, 8, 128), f32),
            pltpu.VMEM((ROW, 1, 128), f32),
            pltpu.VMEM((GR * COL, 1, 128), f32),
            pltpu.VMEM((2, CH, CH), jnp.bfloat16),
            dma((3,)),
            dma((2, 2)),
            dma((16,)),
            dma((16,)),
            dma((ROW - 1,)),
            dma((ROW - 1,)),
            dma((GR * COL - 1,)),
            dma((GR * COL - 1,)),
        ],
        compiler_params=pltpu.CompilerParams(
            collective_id=0, has_side_effects=True, vmem_limit_bytes=32 << 20
        ),
    )(
        pltpu.with_memory_space_constraint(vectors.reshape(NV * RH, CH), pltpu.HBM),
        pltpu.with_memory_space_constraint(disorder, pltpu.HBM),
    )
    anywhere = pl.BlockSpec(memory_space=pl.ANY)
    prev, last, moments = pl.pallas_call(
        store,
        out_shape=(
            jax.ShapeDtypeStruct((NV * RH, CH), f32),
            jax.ShapeDtypeStruct((NV * RH, CH), f32),
            jax.ShapeDtypeStruct((NQ,), f32),
        ),
        in_specs=[anywhere, anywhere, pl.BlockSpec(memory_space=pltpu.VMEM)],
        out_specs=(anywhere, anywhere, anywhere),
        scratch_shapes=[pltpu.VMEM((NQ,), f32), dma((3,))],
        compiler_params=pltpu.CompilerParams(vmem_limit_bytes=1 << 20),
    )(prev, last, moments)
    return prev.reshape(vectors.shape), last.reshape(vectors.shape), moments


def solution(mesh):
    sizes = mesh.shape["grp"], mesh.shape["row"], mesh.shape["col"]
    return jax.shard_map(
        functools.partial(body, sizes),
        mesh=mesh,
        in_specs=(P("grp", "row", "col"), P("row", "col")),
        out_specs=(P("grp", "row", "col"), P("grp", "row", "col"), P()),
        check_vma=False,
    )
```
